32 devices in a mesh: dp: 4 (over z), expert: 8 (over y, x, core).
Axes of the slice: x: 2, y: 2, z: 4, core: 2. Of those that a mesh axis runs over, the one named last changes fastest.
Arguments:
- tokens: bfloat16 [256, 3584], P(('dp', 'expert')), may hold values from -6 to 6
- routes: int32 [256, 8], P(('dp', 'expert')), may hold values from 0 to 63, as said below
- gate_values: bfloat16 [256, 8], P(('dp', 'expert')), may hold values from 0.099609375 to 0.5
- expert_map: int32 [64], replicated, may hold values from 0 to 63, as said below
- row_counts: int32 [32], P(('dp', 'expert')), may hold values from 1 to 8, 224 in all
- gate_weight: bfloat16 [8, 3584, 2048], P('expert', None, 'dp'), may hold values from -0.09375 to 0.09375
- up_weight: bfloat16 [8, 3584, 2048], P('expert', None, 'dp'), may hold values from -0.09375 to 0.09375
- down_weight: bfloat16 [8, 2048, 3584], P('expert', 'dp'), may hold values from -0.125 to 0.125
- delta_in: bfloat16 [8, 8, 3584, 256], P('expert', 'dp'), may hold values from -0.09375 to 0.09375
- delta_out: bfloat16 [8, 8, 256, 3584], P('expert', 'dp'), may hold values from -0.375 to 0.375
Outputs:
- mixed: bfloat16 [256, 3584], P(('dp', 'expert'))
The draws below stay inside these ranges and needn't reach their ends.
Inputs may be any that keep to these rules, and one draw needn't show every extreme that they name: `routes`: each row names 8 different experts, two in each of 4 different bases; at most 8 rows of one device route to one base, and some device has a base that 8 of its rows route to. `expert_map`: A permutation of the 64 slots.
All inputs are finite; a program needn't handle non-finite values. No bound on the sum of `row_counts` on one device may be relied on, other than what follows from the above.
Results may differ from the reference program's by a relative error of at most 0.015.
Values may be sent and summed in bfloat16 or wider, within the bound.
No kernel may reach another device: no remote copies, remote signals or barrier semaphores. Data moves between devices by JAX's collectives and lax.ppermute only.
A program may use at most 64 MiB of HBM per device.

```python
import math
import jax
import jax.numpy as jnp
import numpy as np
from jax import lax

D = 3584
FF = 2048
R = 256
JSLOT = 8
BTOP = 4
TOP = 8
ROWS_DEV = 8
DEVICES_ALL = 32
TOKENS = 256
BASES = 8
CAP = 8
N_DP = 4
N_EXPERT = 8


def route_layout(key):
    base_count = N_EXPERT
    slot_count = JSLOT * base_count
    devices = N_DP * N_EXPERT
    key_list = jax.random.split(jax.random.fold_in(key, 11), 6)
    slot_of_expert = jax.random.permutation(key_list[0], slot_count).astype(jnp.int32)
    expert_of_slot = jnp.argsort(slot_of_expert).astype(jnp.int32)
    base_order = jax.random.permutation(key_list[1], base_count).astype(jnp.int32)
    offset = jax.random.randint(key_list[2], (devices,), 0, base_count // 4 + 1)
    doubled = jax.random.randint(key_list[3], (devices,), 0, 2)
    doubled = jnp.where(jnp.arange(devices) == 0, 0, doubled)
    window = base_count // 2 * (1 + doubled)
    position = jnp.arange(ROWS_DEV)[:, None] * BTOP + jnp.arange(BTOP)[None, :]
    in_window = position[None, :, :] % window[:, None, None]
    chosen_base = base_order[(offset[:, None, None] + in_window) % base_count]
    first_slot = jax.random.randint(key_list[4], (devices, ROWS_DEV, BTOP), 0, JSLOT)
    second = (first_slot + jax.random.randint(key_list[5], (devices, ROWS_DEV, BTOP), 1, JSLOT)) % JSLOT
    slot_ids = chosen_base[:, :, :, None] * JSLOT + jnp.stack([first_slot, second], axis=-1)
    experts = expert_of_slot[slot_ids].reshape(devices * ROWS_DEV, BTOP * 2)
    return (slot_of_expert, experts.astype(jnp.int32))


def draw_routes(key, part):
    return route_layout(key)[1]


def draw_expert_map(key, part):
    return route_layout(key)[0]


def block_levels(rng, dims, cuts, low, top_value):
    factor_of = 1.0
    for dim, parts in cuts:
        draws = jax.random.uniform(jax.random.fold_in(jax.random.fold_in(rng, 6), dim), (parts,), jnp.float32, low / len(cuts), top_value / len(cuts))
        factor_of = factor_of * jnp.repeat(jnp.exp(draws), dims[dim] // parts).reshape((-1,) + (1,) * (len(dims) - 1 - dim))
    return factor_of


def split_up(amount, total, most, skew):
    loads = [(1 << 20) // math.isqrt(rank ** skew) + 1 for rank in range(2, amount + 1)]
    spare, given = total - most - (amount - 1), [1] * (amount - 1)
    while spare > 0:
        movable = [i for i in range(amount - 1) if given[i] < most]
        mass, budget = sum([loads[i] for i in movable]), spare
        for i in movable:
            extra = min(most - given[i], max(1, budget * loads[i] // mass), spare)
            given[i] = given[i] + extra
            spare = spare - extra
    return np.array([most] + given)


def ragged(key, count, total, reach, skew):
    if count == 2:
        one = jax.random.randint(key, (), max(1, total - reach), min(reach, total - 1) + 1)
        return jnp.stack([one, total - one])
    lengths = jnp.asarray(split_up(count, total, reach, skew), jnp.int32)
    pairs = (count - 1) // 2
    donor, receiver = lengths[1:1 + 2 * pairs:2], lengths[2:2 + 2 * pairs:2]
    margin = jnp.minimum(donor - 1, reach - receiver)
    moved = jax.random.randint(jax.random.fold_in(key, 1), (pairs,), 0, 1 << 20) % (margin + 1)
    lengths = lengths.at[1:1 + 2 * pairs:2].set(donor - moved).at[2:2 + 2 * pairs:2].set(receiver + moved)
    return lengths[jax.random.permutation(jax.random.fold_in(key, 2), count)]


def normal_values(key, dims, deviation, reach, cuts=(), held_as=jnp.bfloat16):
    level = block_levels(key, dims, cuts, -0.22, 0.18) if cuts else 1.0
    entries = jax.random.normal(key, dims, jnp.float32) * deviation * level
    return jnp.minimum(jnp.maximum(entries, -reach), reach).astype(held_as)


def setup_inputs(seed: int = 0) -> dict:
    arg_keys = jax.random.split(jax.random.key(seed), 11)
    return {
        "tokens": normal_values(arg_keys[0], (TOKENS, D), 1.0, 6.0, ((0, 32),)),
        "routes": draw_routes(jax.random.fold_in(arg_keys[10], 71), 0),
        "gate_values": jnp.clip(0.099609375 + 0.40039062 * jax.random.uniform(arg_keys[2], (TOKENS, TOP), jnp.float32) ** block_levels(arg_keys[2], (TOKENS, TOP), ((0, 32),), -0.2, 0.2), 0.099609375, 0.5).astype(jnp.bfloat16),
        "expert_map": draw_expert_map(jax.random.fold_in(arg_keys[10], 71), 0),
        "row_counts": ragged(arg_keys[4], DEVICES_ALL, N_DP * N_EXPERT * ROWS_DEV * 7 // 8, ROWS_DEV, 1).astype(jnp.int32),
        "gate_weight": normal_values(arg_keys[5], (BASES, D, FF), D ** -0.5, 0.09375, ((0, 8), (2, 4))),
        "up_weight": normal_values(arg_keys[6], (BASES, D, FF), D ** -0.5, 0.09375, ((0, 8), (2, 4))),
        "down_weight": normal_values(arg_keys[7], (BASES, FF, D), FF ** -0.5, 0.125, ((0, 8), (1, 4))),
        "delta_in": normal_values(arg_keys[8], (BASES, JSLOT, D, R), D ** -0.5, 0.09375, ((0, 8), (1, 4))),
        "delta_out": normal_values(arg_keys[9], (BASES, JSLOT, R, D), R ** -0.5, 0.375, ((0, 8), (1, 4))),
    }


def slot_table(routes, gate_values, expert_map, live_mask):
    experts = expert_map.shape[0]
    identity_ids = jnp.arange(experts, dtype=jnp.int32)
    matches = routes[:, :, None] == identity_ids[None, None, :]
    slot_ids = jnp.sum(jnp.where(matches, expert_map[None, None, :], 0), axis=2).astype(jnp.int32)
    chosen = slot_ids[:, :, None] == identity_ids[None, None, :]
    spread = jnp.sum(jnp.where(chosen, gate_values.astype(jnp.float32)[:, :, None], jnp.float32(0.0)), axis=1)
    spread = jnp.where(live_mask[:, None], spread, jnp.float32(0.0))
    return spread.astype(jnp.bfloat16)


def placement_table(slot_gates, base_count, capacity):
    blocks, row_total, slot_count = slot_gates.shape
    grouped = slot_gates.reshape(blocks, row_total, base_count, slot_count // base_count)
    member = jnp.sum((grouped > 0).astype(jnp.int32), axis=3) > 0
    counted = member.astype(jnp.int32)
    before = jnp.cumsum(counted, axis=1) - counted
    target = jnp.where(member, before, -1)
    return (target[:, :, :, None] == jnp.arange(capacity, dtype=jnp.int32)).astype(jnp.bfloat16)


def slice_term(sent_rows, sent_gates, gate_part, up_part, down_part, in_part, out_part, first_slot):
    slot_span = in_part.shape[0]
    gate_value = jnp.dot(sent_rows, gate_part, preferred_element_type=jnp.float32)
    up_value = jnp.dot(sent_rows, up_part, preferred_element_type=jnp.float32)
    hidden = (jax.nn.silu(gate_value) * up_value).astype(jnp.bfloat16)
    shared = jnp.dot(hidden, down_part, preferred_element_type=jnp.float32)
    gate_total = jnp.sum(sent_gates.astype(jnp.float32), axis=1, keepdims=True)
    own_gates = lax.dynamic_slice_in_dim(sent_gates, first_slot, slot_span, 1).astype(jnp.float32)
    latent = jnp.einsum("nd,jdr->jnr", sent_rows.astype(jnp.float32), in_part.astype(jnp.float32)).astype(jnp.bfloat16)
    lifted = jnp.einsum("jnr,jrd->jnd", latent.astype(jnp.float32), out_part.astype(jnp.float32))
    deltas = jnp.einsum("nj,jnd->nd", own_gates, lifted)
    return gate_total * shared + deltas


def reference(tokens, routes, gate_values, expert_map, row_counts, gate_weight, up_weight, down_weight, delta_in, delta_out):
    devices = N_DP * N_EXPERT
    live_mask = (jnp.arange(ROWS_DEV, dtype=jnp.int32)[None, :] < row_counts[:, None]).reshape(-1)
    slot_gates = slot_table(routes, gate_values, expert_map, live_mask)
    blocked = slot_gates.reshape(devices, ROWS_DEV, JSLOT * N_EXPERT)
    placed = placement_table(blocked, N_EXPERT, CAP).astype(jnp.float32)
    token_blocks = tokens.reshape(devices, ROWS_DEV, D).astype(jnp.float32)
    gate_blocks = blocked.reshape(devices, ROWS_DEV, N_EXPERT, JSLOT).astype(jnp.float32)
    slice_width = FF // N_DP
    slot_span = JSLOT // N_DP

    def one_base(index):
        chosen_rows = placed[:, :, index, :]
        sent_rows = jnp.einsum("nrc,nrd->ncd", chosen_rows, token_blocks).astype(jnp.bfloat16).reshape(devices * CAP, D)
        sent_gates = jnp.einsum("nrc,nrj->ncj", chosen_rows, gate_blocks[:, :, index, :]).astype(jnp.bfloat16).reshape(devices * CAP, JSLOT)
        gate_base = gate_weight[index]
        up_base = up_weight[index]
        down_base = down_weight[index]
        in_base = delta_in[index]
        out_base = delta_out[index]
        total = jnp.zeros((devices * CAP, D), jnp.float32)
        for piece in range(N_DP):
            low_col = piece * slice_width
            high_col = low_col + slice_width
            low_slot = piece * slot_span
            high_slot = low_slot + slot_span
            partial_value = slice_term(sent_rows, sent_gates, gate_base[:, low_col:high_col], up_base[:, low_col:high_col],
                                 down_base[low_col:high_col, :], in_base[low_slot:high_slot], out_base[low_slot:high_slot], low_slot)
            rounded = lax.optimization_barrier(partial_value.astype(jnp.bfloat16))
            total = total + rounded.astype(jnp.float32)
        return total.astype(jnp.bfloat16).reshape(devices, CAP, D)

    results = lax.map(one_base, jnp.arange(N_EXPERT, dtype=jnp.int32))
    mixed = jnp.einsum("nrbc,bncd->nrd", placed, results.astype(jnp.float32))
    return mixed.reshape(devices * ROWS_DEV, D).astype(jnp.bfloat16)
```

```python
import functools

import jax
import jax.numpy as jnp
from jax import lax
from jax.experimental import pallas as pl
from jax.experimental.pallas import tpu as pltpu
from jax.sharding import PartitionSpec as P

JSLOT = 8
BTOP = 4


def slot_table(routes, gate_values, expert_map, live_mask):
    experts = expert_map.shape[0]
    identity_ids = jnp.arange(experts, dtype=jnp.int32)
    matches = routes[:, :, None] == identity_ids[None, None, :]
    slot_ids = jnp.sum(jnp.where(matches, expert_map[None, None, :], 0), axis=2)
    chosen = slot_ids[:, :, None] == identity_ids[None, None, :]
    spread = jnp.sum(
        jnp.where(chosen, gate_values.astype(jnp.float32)[:, :, None], jnp.float32(0.0)), axis=1
    )
    spread = jnp.where(live_mask[:, None], spread, jnp.float32(0.0))
    return spread.astype(jnp.bfloat16)


def placement_table(slot_gates, base_count, capacity):
    blocks, row_total, slot_count = slot_gates.shape
    grouped = slot_gates.reshape(blocks, row_total, base_count, slot_count // base_count)
    member = jnp.sum((grouped > 0).astype(jnp.int32), axis=3) > 0
    counted = member.astype(jnp.int32)
    before = jnp.cumsum(counted, axis=1) - counted
    target = jnp.where(member, before, -1)
    return (target[:, :, :, None] == jnp.arange(capacity, dtype=jnp.int32)).astype(jnp.bfloat16)


def slice_term(sent_rows, sent_gates, gate_part, up_part, down_part, in_part, out_part, first_slot):
    slot_span = in_part.shape[0]
    gate_value = jnp.dot(sent_rows, gate_part, preferred_element_type=jnp.float32)
    up_value = jnp.dot(sent_rows, up_part, preferred_element_type=jnp.float32)
    hidden = (jax.nn.silu(gate_value) * up_value).astype(jnp.bfloat16)
    shared = jnp.dot(hidden, down_part, preferred_element_type=jnp.float32)
    gate_total = jnp.sum(sent_gates.astype(jnp.float32), axis=1, keepdims=True)
    own_gates = lax.dynamic_slice_in_dim(sent_gates, first_slot, slot_span, 1).astype(jnp.float32)
    latent = jnp.einsum(
        "nd,jdr->jnr", sent_rows, in_part, preferred_element_type=jnp.float32
    ).astype(jnp.bfloat16)
    lifted = jnp.einsum("jnr,jrd->jnd", latent, out_part, preferred_element_type=jnp.float32)
    deltas = jnp.einsum("nj,jnd->nd", own_gates, lifted)
    return gate_total * shared + deltas


def body(
    tokens,
    routes,
    gate_values,
    expert_map,
    row_counts,
    gate_weight,
    up_weight,
    down_weight,
    delta_in,
    delta_out,
):
    row_total = tokens.shape[0]
    width = tokens.shape[1]
    dp_size = lax.axis_size("dp")
    expert_size = lax.axis_size("expert")
    slot_count = expert_map.shape[0]
    capacity = 2 * BTOP * row_total // expert_size
    live_mask = jnp.arange(row_total, dtype=jnp.int32) < row_counts[0]
    slot_gates = slot_table(routes, gate_values, expert_map, live_mask)
    own_placed = placement_table(slot_gates[None], expert_size, capacity)[0]
    all_tokens, all_gates = (
        lax.all_gather(tokens, "dp", axis=0, tiled=True),
        lax.all_gather(slot_gates, "dp", axis=0, tiled=True),
    )
    placed = placement_table(
        all_gates.reshape(dp_size, row_total, slot_count), expert_size, capacity
    )
    sent_rows = jnp.einsum(
        "nrbc,nrd->nbcd",
        placed,
        all_tokens.reshape(dp_size, row_total, width),
        preferred_element_type=jnp.float32,
    ).astype(jnp.bfloat16)
    sent_gates = jnp.einsum(
        "nrbc,nrbj->nbcj",
        placed,
        all_gates.reshape(dp_size, row_total, expert_size, JSLOT),
        preferred_element_type=jnp.float32,
    ).astype(jnp.bfloat16)
    got_rows, got_gates = (
        lax.all_to_all(sent_rows, "expert", split_axis=1, concat_axis=1, tiled=True),
        lax.all_to_all(sent_gates, "expert", split_axis=1, concat_axis=1, tiled=True),
    )
    flat_rows = got_rows.reshape(-1, width)
    flat_gates = got_gates.reshape(-1, JSLOT)
    slot_span = JSLOT // dp_size
    first_slot = lax.axis_index("dp") * slot_span
    gate_part = gate_weight[0]
    up_part = up_weight[0]
    down_part = down_weight[0]
    in_part = delta_in[0]
    out_part = delta_out[0]
    summed = lax.psum_scatter(
        slice_term(
            flat_rows, flat_gates, gate_part, up_part, down_part, in_part, out_part, first_slot
        ).astype(jnp.bfloat16),
        "dp",
        scatter_dimension=0,
        tiled=True,
    )
    results = lax.all_to_all(
        summed.reshape(expert_size, capacity, width),
        "expert",
        split_axis=0,
        concat_axis=0,
        tiled=True,
    )
    mixed = jnp.einsum("rbc,bcd->rd", own_placed, results, preferred_element_type=jnp.float32)
    return mixed.astype(jnp.bfloat16)

AXES = ("dp", "expert")
LANES = 128
TILE = 256
CORES = 2


def exchange(value, dp_size, expert_size, dp_bits, expert_bits):
    pairs = [
        (z * expert_size + e, (z ^ dp_bits) * expert_size + (e ^ expert_bits))
        for z in range(dp_size)
        for e in range(expert_size)
    ]
    return lax.ppermute(value, AXES, pairs)


def ffn_kernel(pieces, ids, *refs):
    rows_in, refs = refs[:pieces], refs[pieces:]
    gate_w, up_w, down_w, in_w, out_w = refs[:5]
    outs, (rows, act, scale) = refs[5 : 5 + pieces], refs[5 + pieces :]
    count = rows_in[0].shape[0]
    width, hidden = gate_w.shape
    span, _, rank = in_w.shape
    top = ids.shape[0]
    for p in range(pieces):
        here = slice(p * count, (p + 1) * count)
        rows[here] = rows_in[p][:, :width]
        meta = rows_in[p][:, width:].astype(jnp.float32)
        values = pltpu.roll(meta, LANES - top, 1)
        lane = lax.broadcasted_iota(jnp.int32, meta.shape, 1)
        total = jnp.zeros_like(meta)
        for j in range(JSLOT):
            picked = jnp.where((meta == ids[j]) & (lane < top), values, 0.0)
            total += picked
            if j < span:
                scale[j, here] = jnp.broadcast_to(
                    jnp.sum(picked, axis=1, keepdims=True), meta.shape
                )
        scale[span, here] = jnp.broadcast_to(jnp.sum(total, axis=1, keepdims=True), meta.shape)

    def wide(j, columns):
        return jnp.concatenate([scale[j]] * (columns // LANES), axis=1)

    @pl.loop(0, hidden // TILE)
    def _(i):
        cols = pl.ds(pl.multiple_of(i * TILE, TILE), TILE)
        gate = jnp.dot(rows[...], gate_w[:, cols], preferred_element_type=jnp.float32)
        up = jnp.dot(rows[...], up_w[:, cols], preferred_element_type=jnp.float32)
        value = gate / (1.0 + jnp.exp(-gate)) * up * wide(span, TILE)
        act[:, cols] = value.astype(jnp.bfloat16)

    @pl.loop(0, span)
    def _(j):
        latent = jnp.dot(rows[...], in_w[j], preferred_element_type=jnp.float32)
        cols = pl.ds(pl.multiple_of(hidden + j * rank, LANES), rank)
        act[:, cols] = (latent * wide(j, rank)).astype(jnp.bfloat16)

    @pl.loop(0, width // TILE)
    def _(i):
        cols = pl.ds(pl.multiple_of(i * TILE, TILE), TILE)
        value = jnp.dot(act[:, :hidden], down_w[:, cols], preferred_element_type=jnp.float32)
        for j in range(span):
            low = hidden + j * rank
            value += jnp.dot(
                act[:, low : low + rank], out_w[j, :, cols], preferred_element_type=jnp.float32
            )
        value = value.astype(jnp.bfloat16)
        for p in range(pieces):
            outs[p][:, cols] = value[p * count : (p + 1) * count]


def ffn(ids, rows_in, weights):
    pieces = len(rows_in)
    count = rows_in[0].shape[0]
    width, hidden = weights[0].shape
    span, _, rank = weights[3].shape
    total = pieces * count
    inner = hidden + span * rank
    vmem = pl.BlockSpec(memory_space=pltpu.VMEM)
    weights = [pltpu.with_memory_space_constraint(w, pltpu.VMEM) for w in weights]
    return pl.pallas_call(
        functools.partial(ffn_kernel, pieces),
        out_shape=[jax.ShapeDtypeStruct((count, width), jnp.bfloat16)] * pieces,
        in_specs=[pl.BlockSpec(memory_space=pltpu.SMEM)] + [vmem] * (pieces + 5),
        out_specs=[vmem] * pieces,
        scratch_shapes=[
            pltpu.VMEM((total, width), jnp.bfloat16),
            pltpu.VMEM((total, inner), jnp.bfloat16),
            pltpu.VMEM((span + 1, total, LANES), jnp.float32),
        ],
        compiler_params=pltpu.CompilerParams(vmem_limit_bytes=16 << 20),
        cost_estimate=pl.CostEstimate(
            flops=2 * total * width * (2 * hidden + span * rank + inner),
            bytes_accessed=2 * width * (2 * hidden + span * rank + inner + 2 * total),
            transcendentals=total * hidden,
        ),
    )(ids, *rows_in, *weights)


def add(*terms):
    return sum(term.astype(jnp.float32) for term in terms)


def dense_body(
    tokens,
    routes,
    gate_values,
    expert_map,
    row_counts,
    gate_weight,
    up_weight,
    down_weight,
    delta_in,
    delta_out,
):
    row_total = tokens.shape[0]
    top = routes.shape[1]
    dp_size = lax.axis_size("dp")
    expert_size = lax.axis_size("expert")
    chips = expert_size // CORES
    slot_span = JSLOT // dp_size

    def swap(value, dp_bits=0, chip_bits=0, core_bits=0):
        return exchange(value, dp_size, expert_size, dp_bits, chip_bits * CORES + core_bits)

    live = jnp.arange(row_total, dtype=jnp.int32) < row_counts[0]
    message = jnp.concatenate(
        [
            tokens,
            routes.astype(jnp.bfloat16),
            jnp.where(live[:, None], gate_values, jnp.bfloat16(0.0)),
            jnp.zeros((row_total, LANES - 2 * top), jnp.bfloat16),
        ],
        axis=1,
    )
    column = jnp.concatenate(
        [message] + [swap(message, dp_bits=k) for k in range(1, dp_size)], axis=0
    )
    mine = [column] + [swap(column, chip_bits=k) for k in range(1, chips)]
    theirs = [swap(piece, core_bits=1) for piece in mine]

    first = lax.axis_index("expert") * JSLOT
    shift = lax.axis_index("dp") * slot_span
    slots = first + (shift + jnp.arange(JSLOT, dtype=jnp.int32)) % JSLOT
    experts = jnp.arange(expert_map.shape[0], dtype=jnp.int32)
    ids = jnp.sum(jnp.where(expert_map[None, :] == slots[:, None], experts[None, :], 0), axis=1)
    weights = [gate_weight[0], up_weight[0], down_weight[0], delta_in[0], delta_out[0]]
    partial = ffn(ids.astype(jnp.float32), mine + theirs, weights)

    kept, given = partial[:chips], partial[chips:]
    paired = [
        add(own, swap(other, core_bits=1)).astype(jnp.bfloat16) for own, other in zip(kept, given)
    ]
    summed = add(paired[0], *[swap(paired[k], chip_bits=k) for k in range(1, chips)])
    summed = summed.astype(jnp.bfloat16)
    blocks = [summed[k * row_total : (k + 1) * row_total] for k in range(dp_size)]
    mixed = add(blocks[0], *[swap(blocks[k], dp_bits=k) for k in range(1, dp_size)])
    return mixed.astype(jnp.bfloat16)


def power_of_two(n):
    return n & (n - 1) == 0


def serves_all_rows(mesh):
    dp_size, expert_size = mesh.shape["dp"], mesh.shape["expert"]
    shaped = power_of_two(dp_size) and power_of_two(expert_size) and expert_size >= CORES
    return shaped and JSLOT % dp_size == 0 and 2 * BTOP >= expert_size


def solution(mesh):
    in_specs = (
        P(("dp", "expert"), None),
        P(("dp", "expert"), None),
        P(("dp", "expert"), None),
        P(),
        P(("dp", "expert")),
        P("expert", None, "dp"),
        P("expert", None, "dp"),
        P("expert", "dp", None),
        P("expert", "dp", None, None),
        P("expert", "dp", None, None),
    )
    out_specs = P(("dp", "expert"), None)
    chosen = dense_body if serves_all_rows(mesh) else body
    return jax.shard_map(chosen, mesh=mesh, in_specs=in_specs, out_specs=out_specs, check_vma=False)
```

```python
import functools

import jax
import jax.numpy as jnp
from jax import lax
from jax.experimental import pallas as pl
from jax.experimental.pallas import tpu as pltpu
from jax.sharding import PartitionSpec as P

JSLOT = 8
BTOP = 4


def slot_table(routes, gate_values, expert_map, live_mask):
    experts = expert_map.shape[0]
    identity_ids = jnp.arange(experts, dtype=jnp.int32)
    matches = routes[:, :, None] == identity_ids[None, None, :]
    slot_ids = jnp.sum(jnp.where(matches, expert_map[None, None, :], 0), axis=2)
    chosen = slot_ids[:, :, None] == identity_ids[None, None, :]
    spread = jnp.sum(
        jnp.where(chosen, gate_values.astype(jnp.float32)[:, :, None], jnp.float32(0.0)), axis=1
    )
    spread = jnp.where(live_mask[:, None], spread, jnp.float32(0.0))
    return spread.astype(jnp.bfloat16)


def placement_table(slot_gates, base_count, capacity):
    blocks, row_total, slot_count = slot_gates.shape
    grouped = slot_gates.reshape(blocks, row_total, base_count, slot_count // base_count)
    member = jnp.sum((grouped > 0).astype(jnp.int32), axis=3) > 0
    counted = member.astype(jnp.int32)
    before = jnp.cumsum(counted, axis=1) - counted
    target = jnp.where(member, before, -1)
    return (target[:, :, :, None] == jnp.arange(capacity, dtype=jnp.int32)).astype(jnp.bfloat16)


def slice_term(sent_rows, sent_gates, gate_part, up_part, down_part, in_part, out_part, first_slot):
    slot_span = in_part.shape[0]
    gate_value = jnp.dot(sent_rows, gate_part, preferred_element_type=jnp.float32)
    up_value = jnp.dot(sent_rows, up_part, preferred_element_type=jnp.float32)
    hidden = (jax.nn.silu(gate_value) * up_value).astype(jnp.bfloat16)
    shared = jnp.dot(hidden, down_part, preferred_element_type=jnp.float32)
    gate_total = jnp.sum(sent_gates.astype(jnp.float32), axis=1, keepdims=True)
    own_gates = lax.dynamic_slice_in_dim(sent_gates, first_slot, slot_span, 1).astype(jnp.float32)
    latent = jnp.einsum(
        "nd,jdr->jnr", sent_rows, in_part, preferred_element_type=jnp.float32
    ).astype(jnp.bfloat16)
    lifted = jnp.einsum("jnr,jrd->jnd", latent, out_part, preferred_element_type=jnp.float32)
    deltas = jnp.einsum("nj,jnd->nd", own_gates, lifted)
    return gate_total * shared + deltas


def body(
    tokens,
    routes,
    gate_values,
    expert_map,
    row_counts,
    gate_weight,
    up_weight,
    down_weight,
    delta_in,
    delta_out,
):
    row_total = tokens.shape[0]
    width = tokens.shape[1]
    dp_size = lax.axis_size("dp")
    expert_size = lax.axis_size("expert")
    slot_count = expert_map.shape[0]
    capacity = 2 * BTOP * row_total // expert_size
    live_mask = jnp.arange(row_total, dtype=jnp.int32) < row_counts[0]
    slot_gates = slot_table(routes, gate_values, expert_map, live_mask)
    own_placed = placement_table(slot_gates[None], expert_size, capacity)[0]
    all_tokens, all_gates = (
        lax.all_gather(tokens, "dp", axis=0, tiled=True),
        lax.all_gather(slot_gates, "dp", axis=0, tiled=True),
    )
    placed = placement_table(
        all_gates.reshape(dp_size, row_total, slot_count), expert_size, capacity
    )
    sent_rows = jnp.einsum(
        "nrbc,nrd->nbcd",
        placed,
        all_tokens.reshape(dp_size, row_total, width),
        preferred_element_type=jnp.float32,
    ).astype(jnp.bfloat16)
    sent_gates = jnp.einsum(
        "nrbc,nrbj->nbcj",
        placed,
        all_gates.reshape(dp_size, row_total, expert_size, JSLOT),
        preferred_element_type=jnp.float32,
    ).astype(jnp.bfloat16)
    got_rows, got_gates = (
        lax.all_to_all(sent_rows, "expert", split_axis=1, concat_axis=1, tiled=True),
        lax.all_to_all(sent_gates, "expert", split_axis=1, concat_axis=1, tiled=True),
    )
    flat_rows = got_rows.reshape(-1, width)
    flat_gates = got_gates.reshape(-1, JSLOT)
    slot_span = JSLOT // dp_size
    first_slot = lax.axis_index("dp") * slot_span
    gate_part = gate_weight[0]
    up_part = up_weight[0]
    down_part = down_weight[0]
    in_part = delta_in[0]
    out_part = delta_out[0]
    summed = lax.psum_scatter(
        slice_term(
            flat_rows, flat_gates, gate_part, up_part, down_part, in_part, out_part, first_slot
        ).astype(jnp.bfloat16),
        "dp",
        scatter_dimension=0,
        tiled=True,
    )
    results = lax.all_to_all(
        summed.reshape(expert_size, capacity, width),
        "expert",
        split_axis=0,
        concat_axis=0,
        tiled=True,
    )
    mixed = jnp.einsum("rbc,bcd->rd", own_placed, results, preferred_element_type=jnp.float32)
    return mixed.astype(jnp.bfloat16)

AXES = ("dp", "expert")
LANES = 128
TILE = 256
CORES = 2


def exchange(value, dp_size, expert_size, dp_bits, expert_bits):
    pairs = [
        (z * expert_size + e, (z ^ dp_bits) * expert_size + (e ^ expert_bits))
        for z in range(dp_size)
        for e in range(expert_size)
    ]
    return lax.ppermute(value, AXES, pairs)


def message_kernel(live_rows, tokens, routes, gates, message, route_tile, gate_tile, sems):
    rows, width = tokens.shape
    top = routes.shape[1]
    copies = [
        pltpu.make_async_copy(source, target, sems.at[i])
        for i, (source, target) in enumerate(
            [(routes, route_tile), (gates, gate_tile), (tokens, message.at[:, :width])]
        )
    ]
    for copy in copies:
        copy.start()
    for copy in copies[:2]:
        copy.wait()
    live = lax.broadcasted_iota(jnp.int32, (rows, top), 0) < live_rows[0]
    message[:, width:] = jnp.concatenate(
        [
            route_tile[...].astype(jnp.float32),
            jnp.where(live, gate_tile[...].astype(jnp.float32), 0.0),
            jnp.zeros((rows, LANES - 2 * top), jnp.float32),
        ],
        axis=1,
    ).astype(jnp.bfloat16)
    copies[2].wait()


def in_hbm(*arrays):
    return [pltpu.with_memory_space_constraint(a, pltpu.HBM) for a in arrays]


def build_message(tokens, routes, gate_values, row_counts):
    rows, width = tokens.shape
    return pl.pallas_call(
        message_kernel,
        out_shape=pltpu.VMEM((rows, width + LANES), jnp.bfloat16),
        in_specs=[pl.BlockSpec(memory_space=pltpu.SMEM)]
        + [pl.BlockSpec(memory_space=pltpu.HBM)] * 3,
        out_specs=pl.BlockSpec(memory_space=pltpu.VMEM),
        scratch_shapes=[
            pltpu.VMEM(routes.shape, routes.dtype),
            pltpu.VMEM(gate_values.shape, gate_values.dtype),
            pltpu.SemaphoreType.DMA((3,)),
        ],
        compiler_params=pltpu.CompilerParams(vmem_limit_bytes=2 << 20),
        name="message",
    )(row_counts, *in_hbm(tokens, routes, gate_values))


def fetch_kernel(count, slots_in, *refs):
    sources, targets = refs[:count], refs[count : 2 * count]
    ids, slots, sems = refs[2 * count :]
    ahead = pltpu.make_async_copy(slots_in, slots, sems.at[count])
    ahead.start()
    copies = [
        pltpu.make_async_copy(sources[i].at[0], targets[i], sems.at[i]) for i in range(count)
    ]
    for copy in copies:
        copy.start()
    ahead.wait()
    first = lax.axis_index("expert") * JSLOT
    shift = lax.axis_index("dp") * (JSLOT // lax.axis_size("dp"))

    @pl.loop(0, slots.shape[0])
    def _(e):
        place = slots[e] - first

        @pl.when((place >= 0) & (place < JSLOT))
        def _():
            ids[(place - shift + JSLOT) % JSLOT] = e.astype(jnp.float32)

    for copy in copies:
        copy.wait()


def fetch(expert_map, weights):
    count = len(weights)
    return pl.pallas_call(
        functools.partial(fetch_kernel, count),
        out_shape=[pltpu.VMEM(w.shape[1:], w.dtype) for w in weights]
        + [pltpu.SMEM((JSLOT,), jnp.float32)],
        in_specs=[pl.BlockSpec(memory_space=pltpu.HBM)] * (count + 1),
        out_specs=[pl.BlockSpec(memory_space=pltpu.VMEM)] * count
        + [pl.BlockSpec(memory_space=pltpu.SMEM)],
        scratch_shapes=[
            pltpu.SMEM(expert_map.shape, expert_map.dtype),
            pltpu.SemaphoreType.DMA((count + 1,)),
        ],
        compiler_params=pltpu.CompilerParams(vmem_limit_bytes=1 << 20),
        cost_estimate=pl.CostEstimate(
            flops=0,
            bytes_accessed=sum(w.size * w.dtype.itemsize for w in weights),
            transcendentals=0,
        ),
        name="fetch",
    )(*in_hbm(expert_map, *weights))


def ffn_kernel(pieces, ids, *refs):
    rows_in, refs = refs[:pieces], refs[pieces:]
    gate_w, up_w, down_w, in_w, out_w = refs[:5]
    outs, (rows, act, scale) = refs[5 : 5 + pieces], refs[5 + pieces :]
    count = rows_in[0].shape[0]
    width, hidden = gate_w.shape
    span, _, rank = in_w.shape
    top = ids.shape[0]
    for p in range(pieces):
        here = slice(p * count, (p + 1) * count)
        rows[here] = rows_in[p][:, :width]
        meta = rows_in[p][:, width:].astype(jnp.float32)
        values = pltpu.roll(meta, LANES - top, 1)
        lane = lax.broadcasted_iota(jnp.int32, meta.shape, 1)
        total = jnp.zeros_like(meta)
        for j in range(JSLOT):
            picked = jnp.where((meta == ids[j]) & (lane < top), values, 0.0)
            total += picked
            if j < span:
                scale[j, here] = jnp.broadcast_to(
                    jnp.sum(picked, axis=1, keepdims=True), meta.shape
                )
        scale[span, here] = jnp.broadcast_to(jnp.sum(total, axis=1, keepdims=True), meta.shape)

    def wide(j, columns):
        return jnp.concatenate([scale[j]] * (columns // LANES), axis=1)

    @pl.loop(0, hidden // TILE)
    def _(i):
        cols = pl.ds(pl.multiple_of(i * TILE, TILE), TILE)
        gate = jnp.dot(rows[...], gate_w[:, cols], preferred_element_type=jnp.float32)
        up = jnp.dot(rows[...], up_w[:, cols], preferred_element_type=jnp.float32)
        value = gate / (1.0 + jnp.exp(-gate)) * up * wide(span, TILE)
        act[:, cols] = value.astype(jnp.bfloat16)

    @pl.loop(0, span)
    def _(j):
        latent = jnp.dot(rows[...], in_w[j], preferred_element_type=jnp.float32)
        cols = pl.ds(pl.multiple_of(hidden + j * rank, LANES), rank)
        act[:, cols] = (latent * wide(j, rank)).astype(jnp.bfloat16)

    @pl.loop(0, width // TILE)
    def _(i):
        cols = pl.ds(pl.multiple_of(i * TILE, TILE), TILE)
        value = jnp.dot(act[:, :hidden], down_w[:, cols], preferred_element_type=jnp.float32)
        for j in range(span):
            low = hidden + j * rank
            value += jnp.dot(
                act[:, low : low + rank], out_w[j, :, cols], preferred_element_type=jnp.float32
            )
        value = value.astype(jnp.bfloat16)
        for p in range(pieces):
            outs[p][:, cols] = value[p * count : (p + 1) * count]


def ffn(ids, rows_in, weights):
    pieces = len(rows_in)
    count = rows_in[0].shape[0]
    width, hidden = weights[0].shape
    span, _, rank = weights[3].shape
    total = pieces * count
    inner = hidden + span * rank
    vmem = pl.BlockSpec(memory_space=pltpu.VMEM)
    weights = [pltpu.with_memory_space_constraint(w, pltpu.VMEM) for w in weights]
    return pl.pallas_call(
        functools.partial(ffn_kernel, pieces),
        out_shape=[jax.ShapeDtypeStruct((count, width), jnp.bfloat16)] * pieces,
        in_specs=[pl.BlockSpec(memory_space=pltpu.SMEM)] + [vmem] * (pieces + 5),
        out_specs=[vmem] * pieces,
        scratch_shapes=[
            pltpu.VMEM((total, width), jnp.bfloat16),
            pltpu.VMEM((total, inner), jnp.bfloat16),
            pltpu.VMEM((span + 1, total, LANES), jnp.float32),
        ],
        compiler_params=pltpu.CompilerParams(vmem_limit_bytes=16 << 20),
        cost_estimate=pl.CostEstimate(
            flops=2 * total * width * (2 * hidden + span * rank + inner),
            bytes_accessed=2 * width * (2 * hidden + span * rank + inner + 2 * total),
            transcendentals=total * hidden,
        ),
        name="ffn",
    )(ids, *rows_in, *weights)


def add(*terms):
    return sum(term.astype(jnp.float32) for term in terms)


def dense_body(
    tokens,
    routes,
    gate_values,
    expert_map,
    row_counts,
    gate_weight,
    up_weight,
    down_weight,
    delta_in,
    delta_out,
):
    row_total = tokens.shape[0]
    dp_size = lax.axis_size("dp")
    expert_size = lax.axis_size("expert")
    chips = expert_size // CORES

    def swap(value, dp_bits=0, chip_bits=0, core_bits=0):
        return exchange(value, dp_size, expert_size, dp_bits, chip_bits * CORES + core_bits)

    message = build_message(tokens, routes, gate_values, row_counts)
    column = jnp.concatenate(
        [message] + [swap(message, dp_bits=k) for k in range(1, dp_size)], axis=0
    )
    *weights, ids = fetch(expert_map, [gate_weight, up_weight, down_weight, delta_in, delta_out])
    remote = [swap(column, chip_bits=k) for k in range(1, chips)]
    remote, column, ids = lax.optimization_barrier((remote, column, ids))
    theirs = [swap(column, core_bits=1)] + [swap(piece, core_bits=1) for piece in remote]
    partial = ffn(ids, [column] + remote + theirs, weights)

    kept, given = partial[:chips], partial[chips:]
    paired = [
        add(own, swap(other, core_bits=1)).astype(jnp.bfloat16) for own, other in zip(kept, given)
    ]
    summed = add(paired[0], *[swap(paired[k], chip_bits=k) for k in range(1, chips)])
    summed = summed.astype(jnp.bfloat16)
    blocks = [summed[k * row_total : (k + 1) * row_total] for k in range(dp_size)]
    mixed = add(blocks[0], *[swap(blocks[k], dp_bits=k) for k in range(1, dp_size)])
    return mixed.astype(jnp.bfloat16)


def power_of_two(n):
    return n & (n - 1) == 0


def serves_all_rows(mesh):
    dp_size, expert_size = mesh.shape["dp"], mesh.shape["expert"]
    shaped = power_of_two(dp_size) and power_of_two(expert_size) and expert_size >= CORES
    return shaped and JSLOT % dp_size == 0 and 2 * BTOP >= expert_size


def solution(mesh):
    in_specs = (
        P(("dp", "expert"), None),
        P(("dp", "expert"), None),
        P(("dp", "expert"), None),
        P(),
        P(("dp", "expert")),
        P("expert", None, "dp"),
        P("expert", None, "dp"),
        P("expert", "dp", None),
        P("expert", "dp", None, None),
        P("expert", "dp", None, None),
    )
    out_specs = P(("dp", "expert"), None)
    chosen = dense_body if serves_all_rows(mesh) else body
    return jax.shard_map(chosen, mesh=mesh, in_specs=in_specs, out_specs=out_specs, check_vma=False)
```
